32 devices in a mesh: view: 2 (over y), row: 2 (over x), col: 8 (over z, core).
Axes of the slice: x: 2, y: 2, z: 4, core: 2. Of those that a mesh axis runs over, the one named last changes fastest.
Arguments:
- inputs: bfloat16 [2, 512, 8192], P('view', 'col', 'row'), may hold values from -28 to 28, as said below
- weight: bfloat16 [8192, 8192], P('row', 'col'), may hold values from -0.0625 to 0.0625
Outputs:
- grad_hidden: bfloat16 [2, 512, 8192], P('view', 'col', 'row')
- grad_weight: float32 [8192, 8192], P('row', 'col')
The draws below stay inside these ranges and needn't reach their ends.
Inputs may be any that keep to these rules, and one draw needn't show every extreme that they name: `inputs`: feature activations of the two views of a clip; each feature has its own scale.
All inputs are finite; a program needn't handle non-finite values.
Results may differ from the reference program's by a relative error of at most 0.025.
Values may be sent and summed in bfloat16 or wider, within the bound.
No kernel may reach another device: no remote copies, remote signals or barrier semaphores. Data moves between devices by JAX's collectives and lax.ppermute only.
A program may use at most 128 MiB of HBM per device.

```python
import math
import jax
import jax.numpy as jnp
from jax import lax

D = 8192
BATCH = 512


def draw_inputs(key, part):
    key_base, key_noise, key_scale = jax.random.split(key, 3)
    base = jnp.clip(jax.random.normal(key_base, (BATCH, D), jnp.float32), -4.0, 4.0)
    noise = jnp.clip(jax.random.normal(key_noise, (BATCH, D), jnp.float32), -4.0, 4.0)
    scales = jnp.exp(jax.random.uniform(key_scale, (D,), jnp.float32, math.log(0.5), math.log(5.0)))
    first = base * scales
    second = (0.8 * base + 0.6 * noise) * scales
    return jnp.stack([first, second]).astype(jnp.bfloat16)


def shard_levels(key, shape, cuts, smallest, high):
    def one(axis_at, blocks):
        steps = jax.random.uniform(jax.random.fold_in(jax.random.fold_in(key, 6), axis_at), (blocks,), jnp.float32, smallest / len(cuts), high / len(cuts))
        return jnp.repeat(jnp.exp(steps), shape[axis_at] // blocks).reshape((-1,) + (1,) * (len(shape) - axis_at - 1))

    factor_of = one(*cuts[0])
    for cut in cuts[1:]:
        factor_of = factor_of * one(*cut)
    return factor_of


def gaussian(stream_key, extent, scale, limit, pieces=(), held_as=jnp.bfloat16):
    drawn = scale * jax.random.normal(stream_key, extent, jnp.float32)
    if pieces:
        drawn = drawn * shard_levels(stream_key, extent, pieces, -0.22, 0.18)
    return jnp.clip(drawn, -limit, limit).astype(held_as)


def setup_inputs(seed: int = 0) -> dict:
    arg_keys = jax.random.split(jax.random.key(seed), 3)
    inputs = draw_inputs(jax.random.fold_in(arg_keys[2], 71), 0)
    weight = gaussian(arg_keys[1], (D, D), D ** -0.5, 0.0625, ((0, 2), (1, 8)))
    return dict(inputs=inputs, weight=weight)


off_weight = 0.0051
norm_eps = 1e-05

def normalize(inputs_view, weight):
    pre = jnp.dot(inputs_view, weight, preferred_element_type=jnp.float32)
    mean = lax.optimization_barrier(jnp.mean(pre, axis=0))
    centred = pre - mean
    rstd = lax.rsqrt(lax.optimization_barrier(jnp.mean(centred * centred, axis=0)) + norm_eps)
    return ((centred * rstd).astype(jnp.bfloat16), rstd)

def back_norm(dnorm, normed, rstd):
    normed_f = normed.astype(jnp.float32)
    inner = lax.optimization_barrier(jnp.mean(dnorm * normed_f, axis=0))
    return (rstd * (dnorm - lax.optimization_barrier(jnp.mean(dnorm, axis=0)) - normed_f * inner)).astype(jnp.bfloat16)

def reference(inputs, weight):
    first, rstd_first = normalize(inputs[0], weight)
    second, rstd_second = normalize(inputs[1], weight)
    corr = jnp.dot(first.T, second, preferred_element_type=jnp.float32) / BATCH
    diag = jnp.diagonal(corr)
    corr_b = corr.astype(jnp.bfloat16)
    mixed_first = jnp.dot(second, corr_b.T, preferred_element_type=jnp.float32)
    mixed_second = jnp.dot(first, corr_b, preferred_element_type=jnp.float32)
    scale_diag = 2.0 * (diag - 1.0) - 2.0 * off_weight * diag
    dnorm_first = 2.0 * off_weight * mixed_first + scale_diag * second.astype(jnp.float32)
    dnorm_second = 2.0 * off_weight * mixed_second + scale_diag * first.astype(jnp.float32)
    dpre_first = back_norm(dnorm_first, first, rstd_first)
    dpre_second = back_norm(dnorm_second, second, rstd_second)
    grad_weight = jnp.dot(inputs[0].T, dpre_first, preferred_element_type=jnp.float32) + jnp.dot(inputs[1].T, dpre_second, preferred_element_type=jnp.float32)
    grad_weight = grad_weight / math.sqrt(2.0 * BATCH)
    hidden_first = jnp.dot(dpre_first, weight.T, preferred_element_type=jnp.float32)
    hidden_second = jnp.dot(dpre_second, weight.T, preferred_element_type=jnp.float32)
    grad_hidden = jnp.stack([hidden_first, hidden_second]).astype(jnp.bfloat16)
    return (grad_hidden, grad_weight)
```

```python
import math

import jax
import jax.numpy as jnp
from jax import lax
from jax.sharding import PartitionSpec as P

off_weight = 0.0051
norm_eps = 1e-05


def swap(block, axis, distance):
    count = lax.axis_size(axis)
    return lax.ppermute(block, axis, [(at, at ^ distance) for at in range(count)])


def chip_moves(block, moves):
    route = [(2 * a + core, 2 * b + core) for a, b in moves for core in (0, 1)]
    return lax.ppermute(block, "col", route)


def wide(block):
    return block.astype(jnp.float32)


def narrow(block):
    return block.astype(jnp.bfloat16)


def add(first, second):
    return narrow(wide(first) + wide(second))


def sum_over(block, axis, distance=1):
    while distance < lax.axis_size(axis):
        block = add(block, swap(block, axis, distance))
        distance *= 2
    return block


def in_order(own, other, core):
    first = jnp.where(core == 0, own, other)
    second = jnp.where(core == 0, other, own)
    return jnp.concatenate([first, second], axis=0)


OUTER_PAIRS = [(0, 1), (1, 0), (2, 3), (3, 2)]
MIDDLE = [(1, 2), (2, 1)]
OUTWARD = [(1, 0), (2, 3)]
INWARD = [(0, 1), (3, 2)]


def shards(inputs, weight):
    columns = lax.axis_size("col")
    row = lax.axis_index("row")
    col = lax.axis_index("col")
    core = col % 2
    chip = col // 2
    local = inputs[0]
    share = local.shape[0]
    batch = share * columns
    width = weight.shape[1]
    line = columns == 8

    if line:
        near = chip_moves(local, OUTER_PAIRS)
        middle = chip_moves(local, MIDDLE)
        outward = chip_moves(middle, OUTWARD)
        across = chip_moves(near, MIDDLE)
        last = chip_moves(across, OUTWARD)
        streams = [local, near, middle + outward, across + last]
        low = chip < 2
        chips = [
            chip,
            chip ^ 1,
            jnp.where(low, 2, 1),
            jnp.where(low, 3, 0),
        ]
        starts = [at * (2 * share) for at in chips]
        own_blocks = [in_order(s, swap(s, "col", 1), core) for s in streams]
    else:
        starts = [0]
        own_blocks = [lax.all_gather(local, "col", axis=0, tiled=True)]
        streams = own_blocks

    pre = jnp.zeros((batch, width), jnp.float32)
    pre_other = jnp.zeros((batch, width), jnp.bfloat16)
    for start, block in zip(starts, own_blocks):
        part = narrow(jnp.dot(block, weight, preferred_element_type=jnp.float32))
        total = wide(part)
        distance = 1
        while distance < lax.axis_size("row"):
            total = total + wide(swap(narrow(total), "row", distance))
            distance *= 2
        got = swap(narrow(total), "view", 1)
        pre = lax.dynamic_update_slice(pre, total, (start, 0))
        pre_other = lax.dynamic_update_slice(pre_other, got, (start, 0))

    def normalize(values):
        centred = values - jnp.mean(values, axis=0, keepdims=True)
        rstd = lax.rsqrt(jnp.mean(centred * centred, axis=0, keepdims=True) + norm_eps)
        return narrow(centred * rstd), rstd

    normed, rstd = normalize(pre)
    normed_other, _ = normalize(wide(pre_other))
    normed_f = wide(normed)
    other_f = wide(normed_other)
    diag = jnp.sum(normed_f * other_f, axis=0, keepdims=True) / batch

    rows = batch // lax.axis_size("row")
    mine = lax.dynamic_slice(normed_other, (row * rows, 0), (rows, width))
    gram = lax.dot_general(
        mine, normed_other, (((1,), (1,)), ((), ())), preferred_element_type=jnp.float32
    )
    on_diagonal = (
        lax.broadcasted_iota(jnp.int32, gram.shape, 0) + row * rows
        == lax.broadcasted_iota(jnp.int32, gram.shape, 1)
    )
    gram = narrow(jnp.where(on_diagonal, gram - width, gram))
    half = rows // 2
    keep = lax.dynamic_slice(gram, (core * half, 0), (half, batch))
    give = lax.dynamic_slice(gram, ((1 - core) * half, 0), (half, batch))
    piece = add(keep, swap(give, "col", 1))
    piece = sum_over(piece, "col", 2)
    gram = in_order(piece, swap(piece, "col", 1), core)
    if lax.axis_size("row") == 2:
        gram = in_order(gram, swap(gram, "row", 1), row)
    else:
        gram = lax.all_gather(gram, "row", axis=0, tiled=True)
    mixed = (
        jnp.dot(gram, normed, preferred_element_type=jnp.float32)
        + (width * columns) * normed_f
    ) / batch
    scale_diag = 2.0 * (diag - 1.0) - 2.0 * off_weight * diag
    dnorm = 2.0 * off_weight * mixed + scale_diag * other_f
    inner = jnp.mean(dnorm * normed_f, axis=0, keepdims=True)
    dpre = narrow(
        rstd * (dnorm - jnp.mean(dnorm, axis=0, keepdims=True) - normed_f * inner)
    )

    def back(start, size):
        return narrow(
            lax.dot_general(
                lax.dynamic_slice(dpre, (start, 0), (size, width)),
                weight,
                (((1,), (1,)), ((), ())),
                preferred_element_type=jnp.float32,
            )
        )

    if line:
        def chip_sum(start):
            part = back(start, 2 * share)
            give = lax.dynamic_slice(part, ((1 - core) * share, 0), (share, part.shape[1]))
            keep = lax.dynamic_slice(part, (core * share, 0), (share, part.shape[1]))
            return wide(keep) + wide(swap(give, "col", 1))

        far = chip_sum(starts[3])
        far_in = chip_moves(narrow(far), INWARD)
        far_across = chip_moves(narrow(far + wide(far_in)), MIDDLE)
        mid = chip_sum(starts[2])
        mid_in = chip_moves(narrow(mid), INWARD)
        mid_across = chip_moves(narrow(mid + wide(mid_in)), MIDDLE)
        close = chip_sum(starts[1]) + wide(far_across)
        closed = chip_moves(narrow(close), OUTER_PAIRS)
        grad_hidden = narrow(chip_sum(starts[0]) + wide(closed) + wide(mid_across))
    else:
        grad_hidden = lax.psum_scatter(
            back(0, batch), "col", scatter_dimension=0, tiled=True
        )

    dpre_other = swap(dpre, "view", 1)
    streams, normed_other = lax.optimization_barrier((streams, normed_other))
    other_blocks = []
    for stream in streams:
        got = swap(stream, "view", 1)
        other_blocks.append(in_order(got, swap(got, "col", 1), core) if line else got)
    size = own_blocks[0].shape[0]
    clips = jnp.concatenate(own_blocks + other_blocks, axis=0)
    slopes = jnp.concatenate(
        [
            lax.dynamic_slice(values, (start, 0), (size, width))
            for values in (dpre, dpre_other)
            for start in starts
        ],
        axis=0,
    )
    grad_weight = lax.dot_general(
        clips, slopes, (((0,), (0,)), ((), ())), preferred_element_type=jnp.float32
    ) / math.sqrt(2.0 * batch)
    return (grad_hidden[None], grad_weight)


def solution(mesh):
    return jax.shard_map(
        shards,
        mesh=mesh,
        in_specs=(P("view", "col", "row"), P("row", "col")),
        out_specs=(P("view", "col", "row"), P("row", "col")),
        check_vma=False,
    )
```

```python
import math

import jax
import jax.numpy as jnp
from jax import lax
from jax.sharding import PartitionSpec as P


off_weight = 0.0051
norm_eps = 1e-05


def swap(block, axis, distance):
    count = lax.axis_size(axis)
    return lax.ppermute(block, axis, [(at, at ^ distance) for at in range(count)])


def chip_moves(block, moves):
    route = [(2 * a + core, 2 * b + core) for a, b in moves for core in (0, 1)]
    return lax.ppermute(block, "col", route)


def wide(block):
    return block.astype(jnp.float32)


def narrow(block):
    return block.astype(jnp.bfloat16)


def after(block, *earlier):
    return lax.optimization_barrier((block, *earlier))[0]


def add(first, second):
    return narrow(wide(first) + wide(second))


def sum_over(block, axis, distance=1):
    while distance < lax.axis_size(axis):
        block = add(block, swap(block, axis, distance))
        distance *= 2
    return block


def in_order(own, other, core):
    first = jnp.where(core == 0, own, other)
    second = jnp.where(core == 0, other, own)
    return jnp.concatenate([first, second], axis=0)


OUTER_PAIRS = [(0, 1), (1, 0), (2, 3), (3, 2)]
MIDDLE = [(1, 2), (2, 1)]
OUTWARD = [(1, 0), (2, 3)]
INWARD = [(0, 1), (3, 2)]


def shards(inputs, weight):
    columns = lax.axis_size("col")
    row = lax.axis_index("row")
    col = lax.axis_index("col")
    core = col % 2
    chip = col // 2
    local = inputs[0]
    share = local.shape[0]
    batch = share * columns
    width = weight.shape[1]
    line = columns == 8

    if line:
        halves = jnp.split(local, 2, axis=0)
        near = [chip_moves(part, OUTER_PAIRS) for part in halves]
        middle = [chip_moves(part, MIDDLE) for part in halves]
        across = [chip_moves(part, MIDDLE) for part in near]
        outward = [chip_moves(part, OUTWARD) for part in middle]
        last = [chip_moves(part, OUTWARD) for part in across]
        low = chip < 2
        chips = [
            chip,
            chip ^ 1,
            jnp.where(low, 2, 1),
            jnp.where(low, 3, 0),
        ]
        starts = [at * (2 * share) for at in chips]
        arrivals = [
            (0, 0, [(part,) for part in halves]),
            (1, 0, [(part,) for part in near]),
            (2, 0, list(zip(middle, outward))),
            (3, 0, [(across[0], last[0])]),
            (3, share // 2, [(across[1], last[1])]),
        ]
        places = []
        for at, shift, pieces in arrivals:
            size = len(pieces) * (share // 2)
            places.append(
                [(starts[at] + side * share + shift, size) for side in range(2)]
            )
    else:
        arrivals = [(0, 0, [(lax.all_gather(local, "col", axis=0, tiled=True),)])]
        places = [[(0, batch)]]

    pre = jnp.zeros((batch, width), jnp.float32)
    pre_other = jnp.zeros((batch, width), jnp.bfloat16)
    streams, own_blocks, parts, sent = [], [], [], []
    for at, (place, (_, _, pieces)) in enumerate(zip(places, arrivals)):
        merged = []
        for piece in pieces:
            newest = piece[-1]
            if at >= 1:
                newest = after(newest, parts[at - 1])
            if at >= 2:
                newest = after(newest, sent[at - 2])
            merged.append(piece[0] + newest if len(piece) == 2 else newest)
        stream = jnp.concatenate(merged, axis=0) if len(merged) > 1 else merged[0]
        streams.append(stream)
        block = in_order(stream, swap(stream, "col", 1), core) if line else stream
        own_blocks.append(block)
        product = jnp.dot(block, weight, preferred_element_type=jnp.float32)
        parts.append(narrow(product))
        total = wide(parts[at])
        distance = 1
        while distance < lax.axis_size("row"):
            total = total + wide(swap(narrow(total), "row", distance))
            distance *= 2
        sent.append(narrow(total))
        got = swap(sent[at], "view", 1)
        for side, (start, size) in enumerate(place):
            rows = slice(side * size, (side + 1) * size)
            pre = lax.dynamic_update_slice(pre, total[rows], (start, 0))
            pre_other = lax.dynamic_update_slice(pre_other, got[rows], (start, 0))

    def normalize(values):
        centred = values - jnp.mean(values, axis=0, keepdims=True)
        rstd = lax.rsqrt(jnp.mean(centred * centred, axis=0, keepdims=True) + norm_eps)
        return narrow(centred * rstd), rstd

    normed, rstd = normalize(pre)
    normed_other, _ = normalize(wide(pre_other))
    normed_f = wide(normed)
    other_f = wide(normed_other)
    diag = jnp.sum(normed_f * other_f, axis=0, keepdims=True) / batch

    rows = batch // lax.axis_size("row")
    mine = lax.dynamic_slice(normed_other, (row * rows, 0), (rows, width))
    gram = lax.dot_general(
        mine, normed_other, (((1,), (1,)), ((), ())), preferred_element_type=jnp.float32
    )
    on_diagonal = (
        lax.broadcasted_iota(jnp.int32, gram.shape, 0) + row * rows
        == lax.broadcasted_iota(jnp.int32, gram.shape, 1)
    )
    gram = narrow(jnp.where(on_diagonal, gram - width, gram))
    half = rows // 2
    keep = lax.dynamic_slice(gram, (core * half, 0), (half, batch))
    give = lax.dynamic_slice(gram, ((1 - core) * half, 0), (half, batch))
    piece = add(keep, swap(give, "col", 1))
    piece = sum_over(piece, "col", 2)
    if lax.axis_size("row") == 2:
        across_row = swap(piece, "row", 1)
        pair = jnp.concatenate([piece, across_row], axis=0)
        mate = swap(pair, "col", 1)
        gram = in_order(
            in_order(pair[:half], mate[:half], core),
            in_order(pair[half:], mate[half:], core),
            row,
        )
    else:
        gram = in_order(piece, swap(piece, "col", 1), core)
        gram = lax.all_gather(gram, "row", axis=0, tiled=True)
    mixed = (
        jnp.dot(gram, normed, preferred_element_type=jnp.float32)
        + (width * columns) * normed_f
    ) / batch
    scale_diag = 2.0 * (diag - 1.0) - 2.0 * off_weight * diag
    dnorm = 2.0 * off_weight * mixed + scale_diag * other_f
    inner = jnp.mean(dnorm * normed_f, axis=0, keepdims=True)
    dpre = narrow(
        rstd * (dnorm - jnp.mean(dnorm, axis=0, keepdims=True) - normed_f * inner)
    )

    def back(slope, side, sides):
        tall = weight.shape[0] // sides
        return narrow(
            lax.dot_general(
                slope,
                weight[side * tall : (side + 1) * tall],
                (((1,), (1,)), ((), ())),
                preferred_element_type=jnp.float32,
            )
        )

    if line:
        sides = 2

        def chip_sum(slope, side):
            part = back(slope, side, sides)
            tall = part.shape[1]
            give = lax.dynamic_slice(part, ((1 - core) * share, 0), (share, tall))
            keep = lax.dynamic_slice(part, (core * share, 0), (share, tall))
            got = swap(give, "col", 1)
            return wide(keep) + wide(got)

        sums = [[None] * sides for _ in range(4)]
        for at in (3, 2, 1, 0):
            slope = lax.dynamic_slice(dpre, (starts[at], 0), (2 * share, width))
            for side in range(sides):
                sums[at][side] = chip_sum(slope, side)
        first_out = narrow(sums[3][0])
        late = narrow(sums[0][1])
        results = []
        for side in range(sides):
            far = sums[3][side]
            far_in = chip_moves(narrow(far), INWARD)
            far_across = chip_moves(narrow(far + wide(far_in)), MIDDLE)
            mid = sums[2][side]
            mid_in = chip_moves(narrow(mid), INWARD)
            mid_across = chip_moves(narrow(mid + wide(mid_in)), MIDDLE)
            close = sums[1][side] + wide(far_across)
            closed = chip_moves(narrow(close), OUTER_PAIRS)
            results.append(narrow(sums[0][side] + wide(closed) + wide(mid_across)))
        grad_hidden = jnp.concatenate(results, axis=1)
    else:
        grad_hidden = lax.psum_scatter(
            back(dpre, 0, 1), "col", scatter_dimension=0, tiled=True
        )
        first_out = late = grad_hidden

    dpre_other = swap(after(dpre, first_out), "view", 1)
    clips = list(own_blocks)
    slopes = [
        lax.dynamic_slice(dpre, (start, 0), (size, width))
        for place in places
        for start, size in place
    ]
    for at, stream in enumerate(streams):
        if at >= 2:
            stream = after(stream, pre_other)
        got = swap(stream, "view", 1)
        got = after(got, late)
        if line:
            clips += [got, swap(got, "col", 1)]
            (first, size), (second, _) = places[at]
            order = [
                jnp.where(core == 0, first, second),
                jnp.where(core == 0, second, first),
            ]
        else:
            clips.append(got)
            order, size = [0], batch
        slopes += [
            lax.dynamic_slice(dpre_other, (start, 0), (size, width)) for start in order
        ]
    clips, slopes = jnp.concatenate(clips, axis=0), jnp.concatenate(slopes, axis=0)
    grad_weight = lax.dot_general(
        clips, slopes, (((0,), (0,)), ((), ())), preferred_element_type=jnp.float32
    )
    grad_weight = grad_weight / math.sqrt(2.0 * batch)
    return (grad_hidden[None], grad_weight)


def solution(mesh):
    return jax.shard_map(
        shards,
        mesh=mesh,
        in_specs=(P("view", "col", "row"), P("row", "col")),
        out_specs=(P("view", "col", "row"), P("row", "col")),
        check_vma=False,
    )
```

```python
import math

import jax
import jax.numpy as jnp
from jax import lax
from jax.sharding import PartitionSpec as P


off_weight = 0.0051
norm_eps = 1e-05


def swap(block, axis, distance):
    count = lax.axis_size(axis)
    return lax.ppermute(block, axis, [(at, at ^ distance) for at in range(count)])


def chip_moves(block, moves):
    route = [(2 * a + core, 2 * b + core) for a, b in moves for core in (0, 1)]
    return lax.ppermute(block, "col", route)


def wide(block):
    return block.astype(jnp.float32)


def narrow(block):
    return block.astype(jnp.bfloat16)


def after(block, *earlier):
    return lax.optimization_barrier((block, *earlier))[0]


def add(first, second):
    return narrow(wide(first) + wide(second))


def in_order(own, other, core):
    first = jnp.where(core == 0, own, other)
    second = jnp.where(core == 0, other, own)
    return jnp.concatenate([first, second], axis=0)


OUTER_PAIRS = [(0, 1), (1, 0), (2, 3), (3, 2)]
MIDDLE = [(1, 2), (2, 1)]
OUTWARD = [(1, 0), (2, 3)]
INWARD = [(0, 1), (3, 2)]


def shards(inputs, weight):
    columns = lax.axis_size("col")
    row = lax.axis_index("row")
    col = lax.axis_index("col")
    core = col % 2
    chip = col // 2
    local = inputs[0]
    share = local.shape[0]
    batch = share * columns
    width = weight.shape[1]
    line = columns == 8

    if line:
        own = in_order(local, swap(local, "col", 1), core)
        own_part = narrow(
            jnp.dot(own, weight, preferred_element_type=jnp.float32)
        )
        halves = jnp.split(local, 2, axis=0)
        middle = [chip_moves(part, MIDDLE) for part in halves]
        near = [chip_moves(part, OUTER_PAIRS) for part in halves]
        across = [chip_moves(after(part, own_part), MIDDLE) for part in near]
        outward = [chip_moves(after(part, own_part), OUTWARD) for part in middle]
        last = [chip_moves(part, OUTWARD) for part in across]
        low = chip < 2
        chips = [
            chip,
            chip ^ 1,
            jnp.where(low, 2, 1),
            jnp.where(low, 3, 0),
        ]
        starts = [at * (2 * share) for at in chips]
        arrivals = [
            (0, 0, [(local,)]),
            (1, 0, [(part,) for part in near]),
            (2, 0, list(zip(middle, outward))),
            (3, 0, [(across[0], last[0])]),
            (3, share // 2, [(across[1], last[1])]),
        ]
        places = []
        for at, shift, pieces in arrivals:
            size = sum(piece[0].shape[0] for piece in pieces)
            places.append(
                [(starts[at] + side * share + shift, size) for side in range(2)]
            )
    else:
        arrivals = [(0, 0, [(lax.all_gather(local, "col", axis=0, tiled=True),)])]
        places = [[(0, batch)]]

    pre = jnp.zeros((batch, width), jnp.float32)
    pre_other = jnp.zeros((batch, width), jnp.bfloat16)
    streams, own_blocks, parts, sent, arrived = [], [], [], [], []
    for at, (place, (_, _, pieces)) in enumerate(zip(places, arrivals)):
        merged = []
        for piece in pieces:
            newest = piece[-1]
            if at >= 1:
                newest = after(newest, parts[at - 1])
            if at >= 2:
                newest = after(newest, sent[at - 2])
            merged.append(piece[0] + newest if len(piece) == 2 else newest)
        stream = jnp.concatenate(merged, axis=0) if len(merged) > 1 else merged[0]
        streams.append(stream)
        if line and at == 0:
            block, part = own, own_part
        else:
            block = in_order(stream, swap(stream, "col", 1), core) if line else stream
            part = narrow(jnp.dot(block, weight, preferred_element_type=jnp.float32))
        own_blocks.append(block)
        parts.append(part)
        total = wide(parts[at])
        distance = 1
        while distance < lax.axis_size("row"):
            total = total + wide(swap(narrow(total), "row", distance))
            distance *= 2
        sent.append(narrow(total))
        arrived.append(swap(sent[at], "view", 1))
        for side, (start, size) in enumerate(place):
            rows = slice(side * size, (side + 1) * size)
            pre = lax.dynamic_update_slice(pre, total[rows], (start, 0))
    for at, place in enumerate(places):
        got = after(arrived[at], parts[-1]) if at + 1 < len(places) else arrived[at]
        for side, (start, size) in enumerate(place):
            rows = slice(side * size, (side + 1) * size)
            pre_other = lax.dynamic_update_slice(pre_other, got[rows], (start, 0))

    def normalize(values):
        centred = values - jnp.mean(values, axis=0, keepdims=True)
        rstd = lax.rsqrt(jnp.mean(centred * centred, axis=0, keepdims=True) + norm_eps)
        return narrow(centred * rstd), rstd

    normed, rstd = normalize(pre)
    normed_other, _ = normalize(wide(pre_other))
    normed_f = wide(normed)
    other_f = wide(normed_other)
    diag = jnp.sum(normed_f * other_f, axis=0, keepdims=True) / batch

    rows = batch // lax.axis_size("row")
    mine = lax.dynamic_slice(normed_other, (row * rows, 0), (rows, width))
    gram = lax.dot_general(
        mine, normed_other, (((1,), (1,)), ((), ())), preferred_element_type=jnp.float32
    )
    on_diagonal = (
        lax.broadcasted_iota(jnp.int32, gram.shape, 0) + row * rows
        == lax.broadcasted_iota(jnp.int32, gram.shape, 1)
    )
    gram = narrow(jnp.where(on_diagonal, gram - width, gram))
    half = rows // 2
    keep = lax.dynamic_slice(gram, (core * half, 0), (half, batch))
    give = lax.dynamic_slice(gram, ((1 - core) * half, 0), (half, batch))
    piece = add(keep, swap(give, "col", 1))
    begun = piece
    distance = 2
    while distance < columns:
        moved = swap(piece, "col", distance)
        piece = add(piece, moved)
        distance *= 2
    if lax.axis_size("row") == 2:
        across_row = swap(piece, "row", 1)
        gram = in_order(
            in_order(piece, swap(piece, "col", 1), core),
            in_order(across_row, swap(across_row, "col", 1), core),
            row,
        )
    else:
        gram = in_order(piece, swap(piece, "col", 1), core)
        gram = lax.all_gather(gram, "row", axis=0, tiled=True)
    mixed = (
        jnp.dot(gram, normed, preferred_element_type=jnp.float32)
        + (width * columns) * normed_f
    ) / batch
    scale_diag = 2.0 * (diag - 1.0) - 2.0 * off_weight * diag
    dnorm = 2.0 * off_weight * mixed + scale_diag * other_f
    inner = jnp.mean(dnorm * normed_f, axis=0, keepdims=True)
    dpre = narrow(
        rstd * (dnorm - jnp.mean(dnorm, axis=0, keepdims=True) - normed_f * inner)
    )

    def back(slope, side, sides):
        tall = weight.shape[0] // sides
        return narrow(
            lax.dot_general(
                slope,
                weight[side * tall : (side + 1) * tall],
                (((1,), (1,)), ((), ())),
                preferred_element_type=jnp.float32,
            )
        )

    if line:
        sides = 2

        def chip_sum(slope, side):
            part = back(slope, side, sides)
            tall = part.shape[1]
            give = lax.dynamic_slice(part, ((1 - core) * share, 0), (share, tall))
            keep = lax.dynamic_slice(part, (core * share, 0), (share, tall))
            got = swap(give, "col", 1)
            return wide(keep) + wide(got)

        sums = [[None] * sides for _ in range(4)]
        for at in (3, 2, 1, 0):
            slope = lax.dynamic_slice(dpre, (starts[at], 0), (2 * share, width))
            for side in range(sides):
                sums[at][side] = chip_sum(slope, side)
        results = []
        first_out = narrow(sums[3][0])
        for side in range(sides):
            far = sums[3][side]
            far_in = chip_moves(narrow(far), INWARD)
            far_across = chip_moves(narrow(far + wide(far_in)), MIDDLE)
            mid = sums[2][side]
            mid_in = chip_moves(narrow(mid), INWARD)
            mid_across = chip_moves(narrow(mid + wide(mid_in)), MIDDLE)
            close = sums[1][side] + wide(far_across)
            closed = chip_moves(narrow(close), OUTER_PAIRS)
            late = far_across
            results.append(narrow(sums[0][side] + wide(closed) + wide(mid_across)))
        grad_hidden = jnp.concatenate(results, axis=1)
    else:
        grad_hidden = lax.psum_scatter(
            back(dpre, 0, 1), "col", scatter_dimension=0, tiled=True
        )
        first_out = late = grad_hidden

    dpre_other = swap(after(dpre, first_out), "view", 1)
    clips = [after(block, late) for block in own_blocks]
    slopes = [
        lax.dynamic_slice(dpre, (start, 0), (size, width))
        for place in places
        for start, size in place
    ]
    for at, stream in enumerate(streams):
        stream = after(stream, parts[0] if at == 0 else begun)
        got = swap(stream, "view", 1)
        got = after(got, late)
        if line:
            clips += [got, swap(got, "col", 1)]
            (first, size), (second, _) = places[at]
            order = [
                jnp.where(core == 0, first, second),
                jnp.where(core == 0, second, first),
            ]
        else:
            clips.append(got)
            order, size = [0], batch
        slopes += [
            lax.dynamic_slice(dpre_other, (start, 0), (size, width)) for start in order
        ]
    clips, slopes = jnp.concatenate(clips, axis=0), jnp.concatenate(slopes, axis=0)
    grad_weight = lax.dot_general(
        clips, slopes, (((0,), (0,)), ((), ())), preferred_element_type=jnp.float32
    )
    grad_weight = grad_weight / math.sqrt(2.0 * batch)
    return (grad_hidden[None], grad_weight)


def solution(mesh):
    return jax.shard_map(
        shards,
        mesh=mesh,
        in_specs=(P("view", "col", "row"), P("row", "col")),
        out_specs=(P("view", "col", "row"), P("row", "col")),
        check_vma=False,
    )
```

```python
import math

import jax
import jax.numpy as jnp
from jax import lax
from jax.sharding import PartitionSpec as P


off_weight = 0.0051
norm_eps = 1e-05


def swap(block, axis, distance):
    count = lax.axis_size(axis)
    return lax.ppermute(block, axis, [(at, at ^ distance) for at in range(count)])


def chip_moves(block, moves):
    route = [(2 * a + core, 2 * b + core) for a, b in moves for core in (0, 1)]
    return lax.ppermute(block, "col", route)


def wide(block):
    return block.astype(jnp.float32)


def narrow(block):
    return block.astype(jnp.bfloat16)


def after(block, *earlier):
    return lax.optimization_barrier((block, *earlier))[0]


def add(first, second):
    return narrow(wide(first) + wide(second))


def ordered(own, other, side):
    return [jnp.where(side == 0, own, other), jnp.where(side == 0, other, own)]


def in_order(own, other, side):
    return jnp.concatenate(ordered(own, other, side), axis=0)


OUTER_PAIRS = [(0, 1), (1, 0), (2, 3), (3, 2)]
MIDDLE = [(1, 2), (2, 1)]
OUTWARD = [(1, 0), (2, 3)]
INWARD = [(0, 1), (3, 2)]


def shards(inputs, weight):
    columns = lax.axis_size("col")
    row = lax.axis_index("row")
    col = lax.axis_index("col")
    core = col % 2
    chip = col // 2
    local = inputs[0]
    share = local.shape[0]
    batch = share * columns
    width = weight.shape[1]
    line = columns == 8

    def product(pieces):
        return narrow(
            jnp.dot(
                jnp.concatenate(pieces, axis=0),
                weight,
                preferred_element_type=jnp.float32,
            )
        )

    if line:
        own = ordered(local, swap(local, "col", 1), core)
        own_part = product(own)
        halves = jnp.split(local, 2, axis=0)
        middle, near, outward, across, last = [], [], [], [], []
        for part in halves:
            middle.append(chip_moves(part, MIDDLE))
            near.append(chip_moves(part, OUTER_PAIRS))
        for at in range(2):
            held = after(middle[at], own_part)
            outward.append(chip_moves(held, OUTWARD))
        for at in range(2):
            held = after(near[at], own_part)
            across.append(chip_moves(held, MIDDLE))
        for at in range(2):
            last.append(chip_moves(across[at], OUTWARD))
        low = chip < 2
        chips = [
            chip,
            chip ^ 1,
            jnp.where(low, 2, 1),
            jnp.where(low, 3, 0),
        ]
        starts = [at * (2 * share) for at in chips]
        arrivals = [
            (0, 0, [(local,)]),
            (1, 0, [(part,) for part in near]),
            (2, 0, list(zip(middle, outward))),
            (3, 0, [(across[0], last[0])]),
            (3, share // 2, [(across[1], last[1])]),
        ]
        places = []
        for at, shift, pieces in arrivals:
            size = sum(piece[0].shape[0] for piece in pieces)
            places.append(
                [(starts[at] + side * share + shift, size) for side in range(2)]
            )
    else:
        arrivals = [(0, 0, [(lax.all_gather(local, "col", axis=0, tiled=True),)])]
        places = [[(0, batch)]]

    pre = jnp.zeros((batch, width), jnp.float32)
    pre_other = jnp.zeros((batch, width), jnp.bfloat16)
    streams, own_blocks, parts, sent, arrived = [], [], [], [], []
    for at, (place, (_, _, pieces)) in enumerate(zip(places, arrivals)):
        merged = []
        for piece in pieces:
            newest = piece[-1]
            if at >= 1:
                newest = after(newest, parts[at - 1])
            if at >= 2:
                newest = after(newest, sent[min(at - 2, 1)])
            merged.append(piece[0] + newest if len(piece) == 2 else newest)
        stream = jnp.concatenate(merged, axis=0) if len(merged) > 1 else merged[0]
        streams.append(stream)
        if line and at == 0:
            block, part = own, own_part
        else:
            block = [stream]
            if line:
                block = ordered(stream, swap(stream, "col", 1), core)
            part = product(block)
        own_blocks += block
        parts.append(part)
        total = wide(parts[at])
        distance = 1
        while distance < lax.axis_size("row"):
            total = total + wide(swap(narrow(total), "row", distance))
            distance *= 2
        sent.append(narrow(total))
        arrived.append(swap(sent[at], "view", 1))
        for side, (start, size) in enumerate(place):
            rows = slice(side * size, (side + 1) * size)
            pre = lax.dynamic_update_slice(pre, total[rows], (start, 0))
    for at, place in enumerate(places):
        got = after(arrived[at], parts[-1]) if at + 1 < len(places) else arrived[at]
        for side, (start, size) in enumerate(place):
            rows = slice(side * size, (side + 1) * size)
            pre_other = lax.dynamic_update_slice(pre_other, got[rows], (start, 0))

    def normalize(values):
        centred = values - jnp.mean(values, axis=0, keepdims=True)
        rstd = lax.rsqrt(jnp.mean(centred * centred, axis=0, keepdims=True) + norm_eps)
        return narrow(centred * rstd), rstd

    normed, rstd = normalize(pre)
    normed_other, _ = normalize(wide(pre_other))
    normed_f = wide(normed)
    other_f = wide(normed_other)
    diag = jnp.sum(normed_f * other_f, axis=0, keepdims=True) / batch

    rows = batch // lax.axis_size("row")
    mine = lax.dynamic_slice(normed_other, (row * rows, 0), (rows, width))
    gram = lax.dot_general(
        mine, normed_other, (((1,), (1,)), ((), ())), preferred_element_type=jnp.float32
    )
    on_diagonal = (
        lax.broadcasted_iota(jnp.int32, gram.shape, 0) + row * rows
        == lax.broadcasted_iota(jnp.int32, gram.shape, 1)
    )
    gram = narrow(jnp.where(on_diagonal, gram - width, gram))
    half = rows // 2
    keep = lax.dynamic_slice(gram, (core * half, 0), (half, batch))
    give = lax.dynamic_slice(gram, ((1 - core) * half, 0), (half, batch))
    piece = add(keep, swap(give, "col", 1))
    begun = piece
    distance = 2
    while distance < columns:
        moved = swap(piece, "col", distance)
        piece = add(piece, moved)
        distance *= 2
    if lax.axis_size("row") == 2:
        across_row = swap(piece, "row", 1)
        gram = in_order(
            in_order(piece, swap(piece, "col", 1), core),
            in_order(across_row, swap(across_row, "col", 1), core),
            row,
        )
    else:
        gram = in_order(piece, swap(piece, "col", 1), core)
        gram = lax.all_gather(gram, "row", axis=0, tiled=True)
    mixed = (
        jnp.dot(gram, normed, preferred_element_type=jnp.float32)
        + (width * columns) * normed_f
    ) / batch
    scale_diag = 2.0 * (diag - 1.0) - 2.0 * off_weight * diag
    dnorm = 2.0 * off_weight * mixed + scale_diag * other_f
    inner = jnp.mean(dnorm * normed_f, axis=0, keepdims=True)
    dpre = narrow(
        rstd * (dnorm - jnp.mean(dnorm, axis=0, keepdims=True) - normed_f * inner)
    )

    def back(slope, side, sides):
        tall = weight.shape[0] // sides
        return narrow(
            lax.dot_general(
                slope,
                weight[side * tall : (side + 1) * tall],
                (((1,), (1,)), ((), ())),
                preferred_element_type=jnp.float32,
            )
        )

    if line:
        sides = 2

        def chip_sum(slope, side):
            part = back(slope, side, sides)
            tall = part.shape[1]
            give = lax.dynamic_slice(part, ((1 - core) * share, 0), (share, tall))
            keep = lax.dynamic_slice(part, (core * share, 0), (share, tall))
            got = swap(give, "col", 1)
            return wide(keep) + wide(got)

        sums = [[None] * sides for _ in range(4)]
        for at in (3, 2, 1, 0):
            slope = lax.dynamic_slice(dpre, (starts[at], 0), (2 * share, width))
            for side in range(sides):
                sums[at][side] = chip_sum(slope, side)
        results, late = [], []
        first_out = narrow(sums[3][0])
        for side in range(sides):
            far = sums[3][side]
            far_in = chip_moves(narrow(far), INWARD)
            far_across = chip_moves(narrow(far + wide(far_in)), MIDDLE)
            mid = sums[2][side]
            mid_in = chip_moves(narrow(mid), INWARD)
            mid_across = chip_moves(narrow(mid + wide(mid_in)), MIDDLE)
            close = sums[1][side] + wide(far_across)
            closed = chip_moves(narrow(close), OUTER_PAIRS)
            late.append(far_across)
            results.append(narrow(sums[0][side] + wide(closed) + wide(mid_across)))
        grad_hidden = jnp.concatenate(results, axis=1)
    else:
        grad_hidden = lax.psum_scatter(
            back(dpre, 0, 1), "col", scatter_dimension=0, tiled=True
        )
        first_out, late = grad_hidden, [grad_hidden] * 2

    dpre_other = swap(after(dpre, first_out), "view", 1)
    clips = [after(block, late[0]) for block in own_blocks]
    slopes = [
        lax.dynamic_slice(dpre, (start, 0), (size, width))
        for place in places
        for start, size in place
    ]
    for at, stream in enumerate(streams):
        if at >= 2:
            stream = after(stream, begun)
        got = swap(stream, "view", 1)
        if line:
            clips += [got, swap(got, "col", 1)]
            (first, size), (second, _) = places[at]
            order = [
                jnp.where(core == 0, first, second),
                jnp.where(core == 0, second, first),
            ]
        else:
            clips.append(got)
            order, size = [0], batch
        slopes += [
            lax.dynamic_slice(dpre_other, (start, 0), (size, width)) for start in order
        ]
    clips, slopes = jnp.concatenate(clips, axis=0), jnp.concatenate(slopes, axis=0)
    grad_weight = lax.dot_general(
        clips, slopes, (((0,), (0,)), ((), ())), preferred_element_type=jnp.float32
    )
    grad_weight = grad_weight / math.sqrt(2.0 * batch)
    return (grad_hidden[None], grad_weight)


def solution(mesh):
    return jax.shard_map(
        shards,
        mesh=mesh,
        in_specs=(P("view", "col", "row"), P("row", "col")),
        out_specs=(P("view", "col", "row"), P("row", "col")),
        check_vma=False,
    )
```

```python
import math

import jax
import jax.numpy as jnp
from jax import lax
from jax.sharding import PartitionSpec as P


off_weight = 0.0051
norm_eps = 1e-05


def swap(block, axis, distance):
    count = lax.axis_size(axis)
    return lax.ppermute(block, axis, [(at, at ^ distance) for at in range(count)])


def chip_moves(block, moves):
    route = [(2 * a + core, 2 * b + core) for a, b in moves for core in (0, 1)]
    return lax.ppermute(block, "col", route)


def wide(block):
    return block.astype(jnp.float32)


def narrow(block):
    return block.astype(jnp.bfloat16)


def after(block, *earlier):
    return lax.optimization_barrier((block, *earlier))[0]


def add(first, second):
    return narrow(wide(first) + wide(second))


def in_order(own, other, side):
    first = jnp.where(side == 0, own, other)
    second = jnp.where(side == 0, other, own)
    return jnp.concatenate([first, second], axis=0)


OUTER_PAIRS = [(0, 1), (1, 0), (2, 3), (3, 2)]
MIDDLE = [(1, 2), (2, 1)]
OUTWARD = [(1, 0), (2, 3)]
INWARD = [(0, 1), (3, 2)]


def shards(inputs, weight):
    columns = lax.axis_size("col")
    row = lax.axis_index("row")
    col = lax.axis_index("col")
    core = col % 2
    chip = col // 2
    local = inputs[0]
    share = local.shape[0]
    batch = share * columns
    width = weight.shape[1]
    line = columns == 8

    def product(block):
        return narrow(jnp.dot(block, weight, preferred_element_type=jnp.float32))

    if line:
        own = in_order(local, swap(local, "col", 1), core)
        own_part = product(own)
        halves = jnp.split(local, 2, axis=0)
        middle, near, outward, across, last = [], [], [], [], []
        for part in halves:
            middle.append(chip_moves(part, MIDDLE))
            near.append(chip_moves(part, OUTER_PAIRS))
        for at in range(2):
            held = after(middle[at], own_part)
            outward.append(chip_moves(held, OUTWARD))
        for at in range(2):
            held = after(near[at], own_part)
            across.append(chip_moves(held, MIDDLE))
        for at in range(2):
            last.append(chip_moves(across[at], OUTWARD))
        low = chip < 2
        chips = [
            chip,
            chip ^ 1,
            jnp.where(low, 2, 1),
            jnp.where(low, 3, 0),
        ]
        starts = [at * (2 * share) for at in chips]
        arrivals = [
            (0, 0, [(local,)]),
            (1, 0, [(part,) for part in near]),
            (2, 0, list(zip(middle, outward))),
            (3, 0, [(across[0], last[0])]),
            (3, share // 2, [(across[1], last[1])]),
        ]
        places = []
        for at, shift, pieces in arrivals:
            size = sum(piece[0].shape[0] for piece in pieces)
            places.append(
                [(starts[at] + side * share + shift, size) for side in range(2)]
            )
    else:
        arrivals = [(0, 0, [(lax.all_gather(local, "col", axis=0, tiled=True),)])]
        places = [[(0, batch)]]

    pre = jnp.zeros((batch, width), jnp.float32)
    pre_other = jnp.zeros((batch, width), jnp.bfloat16)
    streams, own_blocks, parts, sent, arrived = [], [], [], [], []
    for at, (place, (_, _, pieces)) in enumerate(zip(places, arrivals)):
        merged = []
        for piece in pieces:
            newest = piece[-1]
            if at >= 1:
                newest = after(newest, parts[at - 1])
            if at >= 2:
                newest = after(newest, sent[min(at - 2, 1)])
            merged.append(piece[0] + newest if len(piece) == 2 else newest)
        stream = jnp.concatenate(merged, axis=0) if len(merged) > 1 else merged[0]
        streams.append(stream)
        if line and at == 0:
            block, part = own, own_part
        else:
            block = stream
            if line:
                block = in_order(stream, swap(stream, "col", 1), core)
            part = product(block)
        own_blocks.append(block)
        parts.append(part)
        total = wide(parts[at])
        distance = 1
        while distance < lax.axis_size("row"):
            total = total + wide(swap(narrow(total), "row", distance))
            distance *= 2
        sent.append(narrow(total))
        arrived.append(swap(sent[at], "view", 1))
        for side, (start, size) in enumerate(place):
            rows = slice(side * size, (side + 1) * size)
            pre = lax.dynamic_update_slice(pre, total[rows], (start, 0))
    for at, place in enumerate(places):
        got = after(arrived[at], parts[-1]) if at + 1 < len(places) else arrived[at]
        for side, (start, size) in enumerate(place):
            rows = slice(side * size, (side + 1) * size)
            pre_other = lax.dynamic_update_slice(pre_other, got[rows], (start, 0))

    def normalize(values):
        centred = values - jnp.mean(values, axis=0, keepdims=True)
        rstd = lax.rsqrt(jnp.mean(centred * centred, axis=0, keepdims=True) + norm_eps)
        return narrow(centred * rstd), rstd

    normed, rstd = normalize(pre)
    normed_other, _ = normalize(wide(pre_other))
    normed_f = wide(normed)
    other_f = wide(normed_other)
    diag = jnp.sum(normed_f * other_f, axis=0, keepdims=True) / batch

    rows = batch // lax.axis_size("row")
    mine = lax.dynamic_slice(normed_other, (row * rows, 0), (rows, width))
    gram = lax.dot_general(
        mine, normed_other, (((1,), (1,)), ((), ())), preferred_element_type=jnp.float32
    )
    on_diagonal = (
        lax.broadcasted_iota(jnp.int32, gram.shape, 0) + row * rows
        == lax.broadcasted_iota(jnp.int32, gram.shape, 1)
    )
    gram = narrow(jnp.where(on_diagonal, gram - width, gram))
    half = rows // 2
    keep = lax.dynamic_slice(gram, (core * half, 0), (half, batch))
    give = lax.dynamic_slice(gram, ((1 - core) * half, 0), (half, batch))
    piece = add(keep, swap(give, "col", 1))
    begun = piece
    distance = 2
    while distance < columns:
        moved = swap(piece, "col", distance)
        piece = add(piece, moved)
        distance *= 2
    if lax.axis_size("row") == 2:
        across_row = swap(piece, "row", 1)
        gram = in_order(
            in_order(piece, swap(piece, "col", 1), core),
            in_order(across_row, swap(across_row, "col", 1), core),
            row,
        )
    else:
        gram = in_order(piece, swap(piece, "col", 1), core)
        gram = lax.all_gather(gram, "row", axis=0, tiled=True)
    mixed = (
        jnp.dot(gram, normed, preferred_element_type=jnp.float32)
        + (width * columns) * normed_f
    ) / batch
    scale_diag = 2.0 * (diag - 1.0) - 2.0 * off_weight * diag
    dnorm = 2.0 * off_weight * mixed + scale_diag * other_f
    inner = jnp.mean(dnorm * normed_f, axis=0, keepdims=True)
    dpre = narrow(
        rstd * (dnorm - jnp.mean(dnorm, axis=0, keepdims=True) - normed_f * inner)
    )

    def back(slope, side, sides):
        tall = weight.shape[0] // sides
        return narrow(
            lax.dot_general(
                slope,
                weight[side * tall : (side + 1) * tall],
                (((1,), (1,)), ((), ())),
                preferred_element_type=jnp.float32,
            )
        )

    if line:
        sides = 2

        def chip_sum(slope, side):
            part = back(slope, side, sides)
            tall = part.shape[1]
            give = lax.dynamic_slice(part, ((1 - core) * share, 0), (share, tall))
            keep = lax.dynamic_slice(part, (core * share, 0), (share, tall))
            got = swap(give, "col", 1)
            return wide(keep) + wide(got)

        sums = [[None] * sides for _ in range(4)]
        for at in (3, 2, 1, 0):
            slope = lax.dynamic_slice(dpre, (starts[at], 0), (2 * share, width))
            for side in range(sides):
                sums[at][side] = chip_sum(slope, side)
        results, late = [], []
        for side in range(sides):
            far = sums[3][side]
            far_in = chip_moves(narrow(far), INWARD)
            mid = sums[2][side]
            far_in = after(far_in, narrow(mid))
            far_across = chip_moves(narrow(far + wide(far_in)), MIDDLE)
            late.append(far_across)
            mid_in = chip_moves(narrow(mid), INWARD)
            mid_across = chip_moves(narrow(mid + wide(mid_in)), MIDDLE)
            close = sums[1][side] + wide(far_across)
            closed = chip_moves(narrow(close), OUTER_PAIRS)
            results.append(narrow(sums[0][side] + wide(closed) + wide(mid_across)))
        grad_hidden = jnp.concatenate(results, axis=1)
    else:
        grad_hidden = lax.psum_scatter(
            back(dpre, 0, 1), "col", scatter_dimension=0, tiled=True
        )
        late = [grad_hidden] * 2

    dpre_other = after(swap(dpre, "view", 1), late[1])
    clips = [after(block, late[0]) for block in own_blocks]
    slopes = [
        lax.dynamic_slice(dpre, (start, 0), (size, width))
        for place in places
        for start, size in place
    ]
    for at, stream in enumerate(streams):
        if at >= 2:
            stream = after(stream, begun)
        got = swap(stream, "view", 1)
        if line:
            clips += [got, swap(got, "col", 1)]
            (first, size), (second, _) = places[at]
            order = [
                jnp.where(core == 0, first, second),
                jnp.where(core == 0, second, first),
            ]
        else:
            clips.append(got)
            order, size = [0], batch
        slopes += [
            lax.dynamic_slice(dpre_other, (start, 0), (size, width)) for start in order
        ]
    clips, slopes = jnp.concatenate(clips, axis=0), jnp.concatenate(slopes, axis=0)
    grad_weight = lax.dot_general(
        clips, slopes, (((0,), (0,)), ((), ())), preferred_element_type=jnp.float32
    )
    grad_weight = grad_weight / math.sqrt(2.0 * batch)
    return (grad_hidden[None], grad_weight)


def solution(mesh):
    return jax.shard_map(
        shards,
        mesh=mesh,
        in_specs=(P("view", "col", "row"), P("row", "col")),
        out_specs=(P("view", "col", "row"), P("row", "col")),
        check_vma=False,
    )
```

```python
import math

import jax
import jax.numpy as jnp
from jax import lax
from jax.sharding import PartitionSpec as P


off_weight = 0.0051
norm_eps = 1e-05


def swap(block, axis, distance):
    count = lax.axis_size(axis)
    return lax.ppermute(block, axis, [(at, at ^ distance) for at in range(count)])


def chip_moves(block, moves):
    route = [(2 * a + core, 2 * b + core) for a, b in moves for core in (0, 1)]
    return lax.ppermute(block, "col", route)


def wide(block):
    return block.astype(jnp.float32)


def narrow(block):
    return block.astype(jnp.bfloat16)


def after(block, *earlier):
    return lax.optimization_barrier((block, *earlier))[0]


def add(first, second):
    return narrow(wide(first) + wide(second))


def in_order(own, other, side):
    first = jnp.where(side == 0, own, other)
    second = jnp.where(side == 0, other, own)
    return jnp.concatenate([first, second], axis=0)


OUTER_PAIRS = [(0, 1), (1, 0), (2, 3), (3, 2)]
MIDDLE = [(1, 2), (2, 1)]
OUTWARD = [(1, 0), (2, 3)]
INWARD = [(0, 1), (3, 2)]


def shards(inputs, weight):
    columns = lax.axis_size("col")
    row = lax.axis_index("row")
    col = lax.axis_index("col")
    core = col % 2
    chip = col // 2
    local = inputs[0]
    share = local.shape[0]
    batch = share * columns
    width = weight.shape[1]
    line = columns == 8

    def product(block):
        return narrow(jnp.dot(block, weight, preferred_element_type=jnp.float32))

    if line:
        own = in_order(local, swap(local, "col", 1), core)
        own_part = product(own)
        halves = jnp.split(local, 2, axis=0)
        middle = chip_moves(local, MIDDLE)
        near = [chip_moves(part, OUTER_PAIRS) for part in halves]
        outward = chip_moves(after(middle, own_part), OUTWARD)
        across, last = [], []
        for at in range(2):
            held = after(near[at], own_part)
            across.append(chip_moves(held, MIDDLE))
        for at in range(2):
            last.append(chip_moves(across[at], OUTWARD))
        low = chip < 2
        chips = [
            chip,
            chip ^ 1,
            jnp.where(low, 2, 1),
            jnp.where(low, 3, 0),
        ]
        starts = [at * (2 * share) for at in chips]
        arrivals = [
            (0, 0, [(local,)]),
            (1, 0, [(part,) for part in near]),
            (2, 0, [(middle, outward)]),
            (3, 0, [(across[0], last[0])]),
            (3, share // 2, [(across[1], last[1])]),
        ]
        places = []
        for at, shift, pieces in arrivals:
            size = sum(piece[0].shape[0] for piece in pieces)
            places.append(
                [(starts[at] + side * share + shift, size) for side in range(2)]
            )
    else:
        arrivals = [(0, 0, [(lax.all_gather(local, "col", axis=0, tiled=True),)])]
        places = [[(0, batch)]]

    pre = jnp.zeros((batch, width), jnp.float32)
    pre_other = jnp.zeros((batch, width), jnp.bfloat16)
    own_blocks, parts, arrived = [], [], []
    for at, (place, (_, _, pieces)) in enumerate(zip(places, arrivals)):
        merged = []
        for piece in pieces:
            newest = piece[-1]
            if at >= 1:
                newest = after(newest, parts[at - 1])
            merged.append(piece[0] + newest if len(piece) == 2 else newest)
        stream = jnp.concatenate(merged, axis=0) if len(merged) > 1 else merged[0]
        if line and at == 0:
            block, part = own, own_part
        else:
            block = stream
            if line:
                block = in_order(stream, swap(stream, "col", 1), core)
            part = product(block)
        own_blocks.append(block)
        parts.append(part)
    for at, place in enumerate(places):
        total = wide(parts[at])
        distance = 1
        while distance < lax.axis_size("row"):
            got = swap(narrow(total), "row", distance)
            if 1 <= at < len(parts) - 1:
                got = after(got, parts[at + 1])
            total = total + wide(got)
            distance *= 2
        arrived.append(swap(narrow(total), "view", 1))
        for side, (start, size) in enumerate(place):
            rows = slice(side * size, (side + 1) * size)
            pre = lax.dynamic_update_slice(pre, total[rows], (start, 0))
    for at, place in enumerate(places):
        got = after(arrived[at], parts[-1]) if at + 1 < len(places) else arrived[at]
        for side, (start, size) in enumerate(place):
            rows = slice(side * size, (side + 1) * size)
            pre_other = lax.dynamic_update_slice(pre_other, got[rows], (start, 0))

    def normalize(values):
        centred = values - jnp.mean(values, axis=0, keepdims=True)
        rstd = lax.rsqrt(jnp.mean(centred * centred, axis=0, keepdims=True) + norm_eps)
        return narrow(centred * rstd), rstd

    normed, rstd = normalize(pre)
    normed_other, _ = normalize(wide(pre_other))
    normed_f = wide(normed)
    other_f = wide(normed_other)
    diag = jnp.sum(normed_f * other_f, axis=0, keepdims=True) / batch

    rows = batch // lax.axis_size("row")
    mine = lax.dynamic_slice(normed_other, (row * rows, 0), (rows, width))
    gram = lax.dot_general(
        mine, normed_other, (((1,), (1,)), ((), ())), preferred_element_type=jnp.float32
    )
    on_diagonal = (
        lax.broadcasted_iota(jnp.int32, gram.shape, 0) + row * rows
        == lax.broadcasted_iota(jnp.int32, gram.shape, 1)
    )
    gram = narrow(jnp.where(on_diagonal, gram - width, gram))
    half = rows // 2
    keep = lax.dynamic_slice(gram, (core * half, 0), (half, batch))
    give = lax.dynamic_slice(gram, ((1 - core) * half, 0), (half, batch))
    piece = add(keep, swap(give, "col", 1))
    begun = piece
    distance = 2
    while distance < columns:
        moved = swap(piece, "col", distance)
        piece = add(piece, moved)
        distance *= 2
    if lax.axis_size("row") == 2:
        across_row = swap(piece, "row", 1)
        gram = in_order(
            in_order(piece, swap(piece, "col", 1), core),
            in_order(across_row, swap(across_row, "col", 1), core),
            row,
        )
    else:
        gram = in_order(piece, swap(piece, "col", 1), core)
        gram = lax.all_gather(gram, "row", axis=0, tiled=True)
    mixed = (
        jnp.dot(gram, normed, preferred_element_type=jnp.float32)
        + (width * columns) * normed_f
    ) / batch
    scale_diag = 2.0 * (diag - 1.0) - 2.0 * off_weight * diag
    dnorm = 2.0 * off_weight * mixed + scale_diag * other_f
    inner = jnp.mean(dnorm * normed_f, axis=0, keepdims=True)
    dpre = narrow(
        rstd * (dnorm - jnp.mean(dnorm, axis=0, keepdims=True) - normed_f * inner)
    )

    def back(slope, side, sides):
        tall = weight.shape[0] // sides
        return narrow(
            lax.dot_general(
                slope,
                weight[side * tall : (side + 1) * tall],
                (((1,), (1,)), ((), ())),
                preferred_element_type=jnp.float32,
            )
        )

    if line:
        sides = 2

        def chip_sum(slope, side):
            part = back(slope, side, sides)
            tall = part.shape[1]
            give = lax.dynamic_slice(part, ((1 - core) * share, 0), (share, tall))
            keep = lax.dynamic_slice(part, (core * share, 0), (share, tall))
            got = swap(give, "col", 1)
            return wide(keep) + wide(got)

        sums = [[None] * sides for _ in range(4)]
        for at in (3, 2, 1, 0):
            slope = lax.dynamic_slice(dpre, (starts[at], 0), (2 * share, width))
            for side in range(sides):
                sums[at][side] = chip_sum(slope, side)
        far_in, mid_in, far_out, far_across = [], [], [], []
        for side in range(sides):
            far = narrow(sums[3][side])
            far_in.append(chip_moves(far, INWARD))
        for side in range(sides):
            mid = narrow(sums[2][side])
            mid_in.append(chip_moves(mid, INWARD))
            got = after(far_in[side], mid)
            far_out.append(narrow(sums[3][side] + wide(got)))
            far_across.append(chip_moves(far_out[side], MIDDLE))

        def merge(total, got):
            return narrow(total + wide(got))

        close = merge(sums[1][0], far_across[0])
        closed = [chip_moves(close, OUTER_PAIRS)]
        mid_out = [merge(sums[2][side], mid_in[side]) for side in range(sides)]
        mid_out = jnp.concatenate(mid_out, axis=1)
        mid_across = chip_moves(mid_out, MIDDLE)
        late = [close, far_across[1]]
        close = merge(sums[1][1], far_across[1])
        closed.append(chip_moves(close, OUTER_PAIRS))
        tall = mid_out.shape[1] // sides
        results = []
        for side in range(sides):
            crossed = mid_across[:, side * tall : (side + 1) * tall]
            results.append(narrow(sums[0][side] + wide(closed[side]) + wide(crossed)))
        grad_hidden = jnp.concatenate(results, axis=1)
    else:
        grad_hidden = lax.psum_scatter(
            back(dpre, 0, 1), "col", scatter_dimension=0, tiled=True
        )
        late = [grad_hidden] * 2

    dpre_other = after(swap(dpre, "view", 1), late[1])
    clips = [after(block, late[0]) for block in own_blocks]
    slopes = [
        lax.dynamic_slice(dpre, (start, 0), (size, width))
        for place in places
        for start, size in place
    ]
    received = []
    for (at, shift, pieces), place in zip(arrivals, places):
        (first, _), (second, _) = place if line else place * 2
        step = 0
        for piece in pieces:
            stream = piece[0] + piece[1] if len(piece) == 2 else piece[0]
            size = stream.shape[0]
            label = len(received)
            if label >= 2:
                stream = after(stream, begun)
            got = swap(stream, "view", 1)
            received.append(got)
            order = [0]
            clips.append(got)
            if line:
                clips.append(swap(got, "col", 1))
                order = [
                    jnp.where(core == 0, first, second) + step,
                    jnp.where(core == 0, second, first) + step,
                ]
            slopes += [
                lax.dynamic_slice(dpre_other, (start, 0), (size, width))
                for start in order
            ]
            step += size
    clips, slopes = jnp.concatenate(clips, axis=0), jnp.concatenate(slopes, axis=0)
    grad_weight = lax.dot_general(
        clips, slopes, (((0,), (0,)), ((), ())), preferred_element_type=jnp.float32
    )
    grad_weight = grad_weight / math.sqrt(2.0 * batch)
    return (grad_hidden[None], grad_weight)


def solution(mesh):
    return jax.shard_map(
        shards,
        mesh=mesh,
        in_specs=(P("view", "col", "row"), P("row", "col")),
        out_specs=(P("view", "col", "row"), P("row", "col")),
        check_vma=False,
    )
```
